256 devices in a mesh: tok: 64 (over y, z, x_hi), out: 4 (over x_lo, core).
Axes of the slice: x: 4 (x_hi: 2, x_lo: 2; x = x_hi * 2 + x_lo), y: 4, z: 8, core: 2. Of those that a mesh axis runs over, the one named last changes fastest.
Arguments:
- acts: bfloat16 [3, 4096, 8192], P(None, 'tok'), may hold values from -6 to 6
- grads: bfloat16 [3, 4096, 4096], P(None, 'tok', 'out'), may hold values from -6 to 6
- act_basis: float32 [1024, 8, 8], P('tok'), may hold values from -2 to 2
- grad_basis: float32 [512, 8, 8], P('out'), may hold values from -2 to 2
Outputs:
- eigen_corr: float32 [4096, 8192], P('out', 'tok')
The draws below stay inside these ranges and needn't reach their ends.
All inputs are finite; a program needn't handle non-finite values.
Results may differ from the reference program's by a relative error of at most 0.014.
Values may be sent and summed in bfloat16 or wider, within the bound.
A program may use at most 128 MiB of HBM per device.

```python
import jax
import jax.numpy as jnp
from jax import lax

DIN = 8192
DOUT = 4096
SEQS = 3
SEQ_LEN = 4096


def levels(key, dims, pieces, low, top_value):
    level = 1.0
    for dim, parts in pieces:
        heights = jax.random.uniform(jax.random.fold_in(jax.random.fold_in(key, 6), dim), (parts,), jnp.float32, low / len(pieces), top_value / len(pieces))
        level = level * jnp.repeat(jnp.exp(heights), dims[dim] // parts).reshape((-1,) + (1,) * (len(dims) - 1 - dim))
    return level


def scatter_about(key, extent, spread, limit, pieces=(), kind=jnp.bfloat16):
    gain = levels(key, extent, pieces, -0.22, 0.18) if pieces else 1.0
    result = jax.random.normal(key, extent, jnp.float32) * spread * gain
    return jnp.minimum(jnp.maximum(result, -limit), limit).astype(kind)


def setup_inputs(seed: int = 0) -> dict:
    seeds = jax.random.split(jax.random.key(seed), 5)
    return {
        "acts": scatter_about(seeds[0], (SEQS, SEQ_LEN, DIN), 1.0, 6.0, ((1, 64),)),
        "grads": scatter_about(seeds[1], (SEQS, SEQ_LEN, DOUT), 1.0, 6.0, ((1, 64), (2, 4))),
        "act_basis": scatter_about(seeds[2], (DIN // 8, 8, 8), 8 ** -0.5, 2.0, ((0, 64),), jnp.float32),
        "grad_basis": scatter_about(seeds[3], (DOUT // 8, 8, 8), 8 ** -0.5, 2.0, ((0, 4),), jnp.float32),
    }


def rotate(values, basis):
    seqs, rows, width = values.shape
    split = values.astype(jnp.float32).reshape(seqs, rows, width // 8, 8)
    turned = jnp.einsum("stbp,bpq->stbq", split, basis.astype(jnp.float32), precision=lax.Precision.HIGHEST)
    return turned.reshape(seqs, rows, width).astype(jnp.bfloat16)


def reference(acts, grads, act_basis, grad_basis):
    rot_acts = rotate(acts, act_basis)
    rot_grads = rotate(grads, grad_basis)
    scale = SEQ_LEN ** -0.5

    def accumulate(total, pair):
        grad_seq, act_seq = pair
        corr = jnp.dot(grad_seq.T, act_seq, preferred_element_type=jnp.float32) * scale
        return total + corr * corr, None

    start_total = jnp.zeros((DOUT, DIN), jnp.float32)
    eigen_corr, unused = lax.scan(accumulate, start_total, (rot_grads, rot_acts))
    return eigen_corr
```

```python
import functools

import jax
import jax.numpy as jnp
from jax import lax
from jax.experimental import pallas as pl
from jax.experimental.pallas import tpu as pltpu
from jax.sharding import PartitionSpec as P

MESH = pl.DeviceIdType.MESH
Y, Z, X = 4, 8, 4
BF16, F32 = jnp.bfloat16, jnp.float32


def gather_kernel(
    acts, grads, out,
    a2, a_all, a_t, g_all, snd, rcv, own, fin, landed,
    a_send, a_recv, w_send, l_send, s_send, g_recv, k_send, k_recv,
    x_send, x_recv, y_send, y_recv, f_send, f_recv, o_sem,
):
    seqs, rows, _ = acts.shape
    width = a2.shape[-1]
    half = width // 2
    tok, place = lax.axis_index("tok"), lax.axis_index("out")
    xh, z, y = lax.rem(tok, 2), lax.rem(lax.div(tok, 2), Z), lax.div(tok, 2 * Z)
    c, xl = lax.rem(place, 2), lax.div(place, 2)
    x = 2 * xh + xl
    sgn = 1 - 2 * c
    chunk = 2 * xl + c

    def dev(xi, yi, zi, ci):
        return ((yi * Z + zi) * 2 + lax.div(xi, 2), 2 * lax.rem(xi, 2) + ci)

    swapped = ((y * Z + z) * 2 + c, 2 * xl + xh)
    stays = xh == c

    def remote(src, dst, send, recv, device):
        return pltpu.make_async_remote_copy(
            src_ref=src, dst_ref=dst, send_sem=send, recv_sem=recv,
            device_id=device, device_id_type=MESH,
        )

    def arrived(ref, sem):
        pltpu.make_async_copy(ref, ref, sem).wait()

    barrier = pltpu.get_barrier_semaphore()

    def greet(device):
        pl.semaphore_signal(barrier, inc=1, device_id=device, device_id_type=MESH)

    @pl.loop(1, Z)
    def _(d):
        greet(dev(x, y, lax.rem(z + d, Z), c))

    @pl.loop(1, Y)
    def _(d):
        greet(dev(x, lax.rem(y + d, Y), z, c))

    @pl.loop(1, 2 * X)
    def _(d):
        greet(dev(lax.rem(x + lax.div(d, 2), X), y, z, lax.rem(c + d, 2)))

    pl.semaphore_wait(barrier, (Z - 1) + (Y - 1) + (2 * X - 1))

    def a2a(s):
        def view(zi):
            col = pl.multiple_of((chunk * Z + zi) * width, width)
            return acts.at[s, :, pl.ds(col, width)]

        @pl.loop(1, Z)
        def _(d):
            zt = lax.rem(z + d, Z)
            remote(view(zt), a2.at[s, z], a_send.at[s, d], a_recv.at[s, z],
                   dev(x, y, zt, c)).start()

        pltpu.make_async_copy(view(z), a2.at[s, z], a_recv.at[s, z]).start()

    def to_swapped(s, wait=False):
        copy = remote(grads.at[s], g_all.at[s, xh, z], w_send.at[s], g_recv.at[s, z], swapped)
        if wait:
            @pl.when(jnp.logical_not(stays))
            def _():
                copy.wait_send()
            return

        @pl.when(stays)
        def _():
            pltpu.make_async_copy(grads.at[s], g_all.at[s, c, z], g_recv.at[s, z]).start()

        @pl.when(jnp.logical_not(stays))
        def _():
            copy.start()

    def block(k):
        return lax.rem(z + k * sgn + Z, Z)

    def ring(s, zz, direction, sem):
        return remote(g_all.at[s, c, zz], g_all.at[s, c, zz], sem, g_recv.at[s, zz],
                      dev(x, y, lax.rem(z + direction + Z, Z), c))

    def long(s, k):
        return ring(s, block(-k), sgn, l_send.at[s, k])

    def short(s, k):
        return ring(s, block(k), -sgn, s_send.at[s, k])

    def across(s, zz):
        return remote(g_all.at[s, c, zz], g_all.at[s, c, zz], k_send.at[s, zz], k_recv.at[s, zz],
                      dev(x, y, z, 1 - c))

    def ring_start(s):
        arrived(g_all.at[s, c, z], g_recv.at[s, z])
        long(s, 0).start()
        short(s, 0).start()
        across(s, z).start()

    def ring_rest(s):
        for k in range(1, 5):
            zz = block(-k)
            arrived(g_all.at[s, c, zz], g_recv.at[s, zz])
            if k < 4:
                long(s, k).start()
            across(s, zz).start()
            if k < 4:
                zz = block(k)
                arrived(g_all.at[s, c, zz], g_recv.at[s, zz])
                if k < 3:
                    short(s, k).start()
                across(s, zz).start()

    def x_copy(s, d):
        h = lax.rem(c + d, 2)
        cols = pl.ds(pl.multiple_of(h * half, half), half)
        return remote(a2.at[s, :, :, cols], a_all.at[s, chunk, xh], x_send.at[s, d],
                      x_recv.at[s, chunk, xh], dev(lax.rem(x + lax.div(d, 2), X), y, z, h))

    def xsend(s):
        @pl.loop(0, Z)
        def _(zz):
            arrived(a2.at[s, zz], a_recv.at[s, zz])

        @pl.loop(1, 2 * X)
        def _(d):
            x_copy(s, d).start()

        cols = pl.ds(pl.multiple_of(c * half, half), half)
        pltpu.make_async_copy(a2.at[s, :, :, cols], a_all.at[s, chunk, xh],
                              x_recv.at[s, chunk, xh]).start()

    def y_copy(s, d):
        yt = lax.rem(y + d, Y)
        return remote(snd.at[s, yt], rcv.at[s, y], y_send.at[s, d], y_recv.at[s, y],
                      dev(x, yt, z, c))

    def compute(s):
        depth = 2 * Z * rows
        for yi in range(Y):
            for t in range(2):
                arrived(a_all.at[s, yi, t], x_recv.at[s, yi, t])
            a_t[yi * half:(yi + 1) * half, :] = a_all[s, yi].reshape(depth, half).T

        @pl.loop(0, Z)
        def _(zz):
            arrived(g_all.at[s, 1 - c, zz], k_recv.at[s, zz])

        @pl.loop(0, 4)
        def _(n):
            cols = pl.ds(pl.multiple_of(n * 256, 256), 256)
            g = g_all[s, :, :, :, cols].reshape(depth, 256)
            r = jnp.dot(a_t[...], g, preferred_element_type=F32)
            for yi in range(Y):
                piece = r[yi * half:(yi + 1) * half]
                snd[s, yi, :, cols] = piece.astype(BF16)

                @pl.when(y == yi)
                def _():
                    own[s, :, cols] = piece

        for d in (2, 1, 3):
            y_copy(s, d).start()

    def f_copy(s):
        return remote(fin.at[s], landed.at[s], f_send.at[s], f_recv.at[s], swapped)

    def reduce(s):
        for d in (1, 3, 2):
            yt = lax.rem(y + d, Y)
            arrived(rcv.at[s, yt], y_recv.at[s, yt])

        @pl.loop(0, half // 16)
        def _(i):
            part = pl.ds(pl.multiple_of(i * 16, 16), 16)
            total = own[s, part, :]
            for d in range(1, Y):
                total = total + rcv[s, lax.rem(y + d, Y), part, :].astype(F32)
            fin[s, part, :] = total.astype(BF16)

        @pl.when(stays)
        def _():
            pltpu.make_async_copy(fin.at[s], landed.at[s], f_recv.at[s]).start()

        @pl.when(jnp.logical_not(stays))
        def _():
            f_copy(s).start()

    for s in range(seqs):
        to_swapped(s)
    a2a(0)
    ring_start(0)
    a2a(1)
    xsend(0)
    ring_rest(0)
    ring_start(1)
    a2a(2)
    xsend(1)
    compute(0)
    ring_rest(1)
    ring_start(2)
    xsend(2)
    compute(1)
    ring_rest(2)
    reduce(0)
    compute(2)
    reduce(1)
    reduce(2)
    for s in range(seqs):
        arrived(landed.at[s], f_recv.at[s])
        pltpu.make_async_copy(landed.at[s], out.at[s], o_sem.at[s]).start()

    @pl.loop(0, seqs)
    def _(s):
        to_swapped(s, wait=True)

        @pl.loop(1, Z)
        def _(d):
            col = pl.multiple_of(chunk * width, width)
            remote(acts.at[s, :, pl.ds(col, width)], a2.at[s, z], a_send.at[s, d],
                   a_recv.at[s, z], swapped).wait_send()

        for k in range(4):
            long(s, k).wait_send()
            if k < 3:
                short(s, k).wait_send()

        @pl.loop(0, Z)
        def _(zz):
            across(s, zz).wait_send()

        @pl.loop(1, 2 * X)
        def _(d):
            x_copy(s, d).wait_send()

        @pl.loop(1, Y)
        def _(d):
            y_copy(s, d).wait_send()

        @pl.when(jnp.logical_not(stays))
        def _():
            f_copy(s).wait_send()

        pltpu.make_async_copy(landed.at[s], out.at[s], o_sem.at[s]).wait()


def gathered(acts, grads):
    seqs, rows, _ = acts.shape
    units = grads.shape[2]
    width = acts.shape[2] // (Y * Z)
    half = width // 2
    dma = pltpu.SemaphoreType.DMA
    return pl.pallas_call(
        gather_kernel,
        out_shape=jax.ShapeDtypeStruct((seqs, half, units), BF16),
        in_specs=[pl.BlockSpec(memory_space=pl.ANY)] * 2,
        out_specs=pl.BlockSpec(memory_space=pl.ANY),
        scratch_shapes=[
            pltpu.VMEM((seqs, Z, rows, width), BF16),
            pltpu.VMEM((seqs, Y, 2, Z, rows, half), BF16),
            pltpu.VMEM((Y * half, 2 * Z * rows), BF16),
            pltpu.VMEM((seqs, 2, Z, rows, units), BF16),
            pltpu.VMEM((seqs, Y, half, units), BF16),
            pltpu.VMEM((seqs, Y, half, units), BF16),
            pltpu.VMEM((seqs, half, units), F32),
            pltpu.VMEM((seqs, half, units), BF16),
            pltpu.VMEM((seqs, half, units), BF16),
            dma((seqs, Z)), dma((seqs, Z)), dma((seqs,)),
            dma((seqs, 4)), dma((seqs, 3)), dma((seqs, Z)),
            dma((seqs, Z)), dma((seqs, Z)),
            dma((seqs, 2 * X)), dma((seqs, Y, 2)),
            dma((seqs, Y)), dma((seqs, Y)),
            dma((seqs,)), dma((seqs,)), dma((seqs,)),
        ],
        compiler_params=pltpu.CompilerParams(
            collective_id=0, has_side_effects=True, vmem_limit_bytes=56 << 20
        ),
        name="gathered",
    )(acts, grads)


def halves(v):
    high = v.astype(BF16)
    return high, (v - high.astype(F32)).astype(BF16)


def dot(a, b):
    return jnp.dot(a, b, preferred_element_type=F32)


def spread(basis):
    lane = lax.broadcasted_iota(jnp.int32, (8, 128), 1)
    pick = (lax.rem(lane, 8) == lax.broadcasted_iota(jnp.int32, (8, 128), 0)).astype(BF16)
    row = lax.div(lax.broadcasted_iota(jnp.int32, (128, 128), 0), 8)
    col = lax.div(lax.broadcasted_iota(jnp.int32, (128, 128), 1), 8)
    return [jnp.where(row == col, dot(part, pick), 0.0).astype(BF16) for part in halves(basis)]


def turn_kernel(corr, act_basis, grad_basis, out, *, scale):
    seqs, half, units = corr.shape
    act_high, act_low = spread(act_basis[...])
    act_high, act_low = act_high.T, act_low.T
    for j in range(units // 128):
        cols = slice(j * 128, (j + 1) * 128)
        grad_high, grad_low = spread(grad_basis[cols, :])
        total = jnp.zeros((half, 128), F32)
        for s in range(seqs):
            piece = corr[s, :, cols]
            high, low = halves(dot(piece, grad_high) + dot(piece, grad_low))
            turned = dot(act_high, high) + (dot(act_high, low) + dot(act_low, high))
            turned = turned * scale
            total = total + turned * turned
        out[cols, :] = total.T


def shards(acts, grads, act_basis, grad_basis):
    corr = gathered(acts, grads)
    length = acts.shape[1] * Y * Z * 2
    units = grads.shape[2]
    half = corr.shape[1]
    return pl.pallas_call(
        functools.partial(turn_kernel, scale=length ** -0.5),
        out_shape=jax.ShapeDtypeStruct((units, half), F32),
        name="turned",
    )(corr, act_basis.reshape(half, 8), grad_basis.reshape(units, 8))


def solution(mesh):
    placed = (
        P(None, "tok", None),
        P(None, "tok", "out"),
        P("tok", None, None),
        P("out", None, None),
    )
    return jax.shard_map(
        shards, mesh=mesh, in_specs=placed, out_specs=P("out", "tok"), check_vma=False
    )
```

```python
import functools

import jax
import jax.numpy as jnp
from jax import lax
from jax.experimental import pallas as pl
from jax.experimental.pallas import tpu as pltpu
from jax.sharding import PartitionSpec as P

MESH = pl.DeviceIdType.MESH
Y, Z, X = 4, 8, 4
PIECE = 256
BF16, F32 = jnp.bfloat16, jnp.float32


def halves(v):
    high = v.astype(BF16)
    return high, (v - high.astype(F32)).astype(BF16)


def dot(a, b):
    return jnp.dot(a, b, preferred_element_type=F32)


def iota(shape, dim):
    return lax.broadcasted_iota(jnp.int32, shape, dim)


def spread(flat, j, size):
    blocks = flat.shape[1]
    first = j * (size // 8)
    repeat = (iota((size, blocks), 1) == first + lax.div(iota((size, blocks), 0), 8)).astype(BF16)
    mine = lax.div(iota((size, 64), 1), 8) == lax.rem(iota((size, 64), 0), 8)
    fold = (lax.rem(iota((64, size), 1), 8) == lax.rem(iota((64, size), 0), 8)).astype(BF16)
    diagonal = lax.div(iota((size, size), 0), 8) == lax.div(iota((size, size), 1), 8)
    parts = []
    for part in halves(flat):
        rows = lax.dot_general(repeat, part, (((1,), (1,)), ((), ())), preferred_element_type=F32)
        rows = jnp.where(mine, rows, 0.0).astype(BF16)
        parts.append(jnp.where(diagonal, dot(rows, fold), 0.0).astype(BF16))
    return parts


def kernel(
    acts, grads, act_basis, grad_basis, out,
    a2, a_all, a_t, g_all, snd, rly, rcv, nxt, own, fin, landed, acc, result, act_flat, grad_flat, act_diag, grad_diag,
    a_send, a_recv, w_send, r_send, g_recv, k_send, k_recv,
    x_send, x_recv, v_send, q_send, q_recv, y_send, y_recv, f_send, f_recv, b_sem, o_sem,
    *, scale,
):
    seqs, rows, _ = acts.shape
    units = grads.shape[2]
    pieces = units // PIECE
    stages = seqs * pieces
    width = a2.shape[-1]
    half = width // 2
    depth = 2 * Z * rows
    tok, place = lax.axis_index("tok"), lax.axis_index("out")
    xh, z, y = lax.rem(tok, 2), lax.rem(lax.div(tok, 2), Z), lax.div(tok, 2 * Z)
    c, xl = lax.rem(place, 2), lax.div(place, 2)
    x = 2 * xh + xl
    sgn = 1 - 2 * c
    chunk = 2 * xl + c

    def dev(xi, yi, zi, ci):
        return ((yi * Z + zi) * 2 + lax.div(xi, 2), 2 * lax.rem(xi, 2) + ci)

    swapped = ((y * Z + z) * 2 + c, 2 * xl + xh)
    stays = xh == c
    moves = jnp.logical_not(stays)

    def remote(src, dst, send, recv, device):
        return pltpu.make_async_remote_copy(
            src_ref=src, dst_ref=dst, send_sem=send, recv_sem=recv,
            device_id=device, device_id_type=MESH,
        )

    def local(src, dst, sem):
        return pltpu.make_async_copy(src, dst, sem)

    def arrived(ref, sem):
        local(ref, ref, sem).wait()

    local(act_basis, act_flat, b_sem.at[0]).start()
    local(grad_basis, grad_flat, b_sem.at[1]).start()
    barrier = pltpu.get_barrier_semaphore()

    def greet(device):
        pl.semaphore_signal(barrier, inc=1, device_id=device, device_id_type=MESH)

    @pl.loop(1, Z)
    def _(d):
        greet(dev(x, y, lax.rem(z + d, Z), c))

    @pl.loop(1, Y)
    def _(d):
        greet(dev(x, lax.rem(y + d, Y), z, c))

    @pl.loop(1, 2 * X)
    def _(d):
        greet(dev(lax.rem(x + lax.div(d, 2), X), y, z, lax.rem(c + d, 2)))

    pl.semaphore_wait(barrier, (Z - 1) + (Y - 1) + (2 * X - 1))

    def a2a_view(s, zt):
        return acts.at[s, :, pl.ds(pl.multiple_of((chunk * Z + zt) * width, width), width)]

    def a2a(s, d):
        for step in {d, Z - d}:
            zt = lax.rem(z + step, Z)
            remote(a2a_view(s, zt), a2.at[s, z], a_send.at[s], a_recv.at[s, z], dev(x, y, zt, c)).start()

    def grads_view(j):
        s, h = lax.div(j, pieces), lax.rem(j, pieces)
        return grads.at[s, :, pl.ds(pl.multiple_of(h * PIECE, PIECE), PIECE)]

    def block(k):
        return lax.rem(z + k * sgn + Z, Z)

    def ring(j, zz, direction, sem):
        return remote(g_all.at[j, c, zz], g_all.at[j, c, zz], sem, g_recv.at[j, zz],
                      dev(x, y, lax.rem(z + direction + Z, Z), c))

    def long(j, k):
        return ring(j, block(-k), sgn, r_send.at[j])

    def short(j, k):
        return ring(j, block(k), -sgn, r_send.at[j])

    def across(j):
        return remote(g_all.at[j, c], g_all.at[j, c], k_send.at[j], k_recv.at[j], dev(x, y, z, 1 - c))

    def hop(j, k):
        zz = block(-k)
        arrived(g_all.at[j, c, zz], g_recv.at[j, zz])
        if k < 4:
            long(j, k).start()
            if k > 0:
                zz = block(k)
                arrived(g_all.at[j, c, zz], g_recv.at[j, zz])
            if k < 3:
                short(j, k).start()
        else:
            across(j).start()

    def x_copy(s, d):
        h = lax.rem(c + d, 2)
        cols = pl.ds(pl.multiple_of(h * half, half), half)
        return remote(a2.at[s, :, :, cols], a_all.at[s, 2 * chunk + xh], x_send.at[s],
                      x_recv.at[s, 2 * chunk + xh], dev(lax.rem(x + lax.div(d, 2), X), y, z, h))

    direct = (2, 3, 6, 7, 1)

    def xsend(s):
        @pl.loop(0, Z)
        def _(zz):
            arrived(a2.at[s, zz], a_recv.at[s, zz])

        for d in direct:
            x_copy(s, d).start()

        cols = pl.ds(pl.multiple_of(c * half, half), half)
        local(a2.at[s, :, :, cols], a_all.at[s, 2 * chunk + xh], x_recv.at[s, 2 * chunk + xh]).start()

    def slot(dx, ci):
        xi = lax.rem(x + dx, X)
        return 2 * (2 * lax.rem(xi, 2) + ci) + lax.div(xi, 2)

    passing = ((X - 1, 0, 1), (1, 1, X - 1))

    def pass_copy(s, i):
        dx, ci, to = passing[i]
        u = slot(dx, ci)
        return remote(a_all.at[s, u], a_all.at[s, u], v_send.at[s, i], x_recv.at[s, u],
                      dev(lax.rem(x + to, X), y, z, c))

    def xpass(s):
        for i, (dx, ci, to) in enumerate(passing):
            u = slot(dx, ci)
            arrived(a_all.at[s, u], x_recv.at[s, u])
            pass_copy(s, i).start()

    def xrest(s):
        for dx in range(X):
            for ci in range(2):
                if (dx, ci) in ((X - 1, 0), (1, 1)):
                    continue
                u = slot(dx, ci)
                arrived(a_all.at[s, u], x_recv.at[s, u])
        for i, yi in enumerate((far, behind, ahead, y)):
            a_t[i * half:(i + 1) * half, :] = a_all[s, pl.ds(2 * yi, 2)].reshape(depth, half).T

    ahead, behind, far = lax.rem(y + sgn + Y, Y), lax.rem(y - sgn + Y, Y), lax.rem(y + 2, Y)

    def far_copy(j):
        return remote(snd.at[j, 0], rly.at[j], q_send.at[j], q_recv.at[j], dev(x, ahead, z, c))

    def behind_copy(j):
        return remote(snd.at[j, 1], rcv.at[j, 0], y_send.at[j, 0], y_recv.at[j, 0], dev(x, behind, z, c))

    def ahead_copy(j):
        return remote(snd.at[j, 2], rcv.at[j, 1], y_send.at[j, 1], y_recv.at[j, 1], dev(x, ahead, z, c))

    def multiply(j):
        @pl.when(lax.rem(j, pieces) == 0)
        def _():
            xrest(lax.div(j, pieces))

        arrived(g_all.at[j, 1 - c], k_recv.at[j])
        product = dot(a_t[...], g_all[j].reshape(depth, PIECE))
        snd[j, 0] = product[:half].astype(BF16)
        snd[j, 1] = product[half:2 * half].astype(BF16)
        nxt[j] = product[2 * half:3 * half]
        own[j] = product[3 * half:]
        far_copy(j).start()
        behind_copy(j).start()

    def relay(j):
        arrived(rly.at[j], q_recv.at[j])
        snd[j, 2] = (nxt[j] + rly[j].astype(F32)).astype(BF16)
        ahead_copy(j).start()

    def f_copy(j):
        return remote(fin.at[j], landed.at[j], f_send.at[j], f_recv.at[j], swapped)

    def reduce(j):
        for i in range(2):
            arrived(rcv.at[j, i], y_recv.at[j, i])
        total = own[j] + (rcv[j, 0].astype(F32) + rcv[j, 1].astype(F32))
        fin[j] = total.astype(BF16)

        @pl.when(stays)
        def _():
            local(fin.at[j], landed.at[j], f_recv.at[j]).start()

        @pl.when(moves)
        def _():
            f_copy(j).start()

    def out_copy(h):
        view = pl.ds(pl.multiple_of(h * PIECE, PIECE), PIECE)
        return local(result.at[view], out.at[view], o_sem.at[h])

    def finish(j):
        s, h = lax.div(j, pieces), lax.rem(j, pieces)
        arrived(landed.at[j], f_recv.at[j])
        piece = landed[j]
        high, low = halves(dot(jnp.concatenate([piece, piece], axis=1), grad_diag[h]))
        turned = dot(act_diag[...], jnp.concatenate([high, low, high], axis=0)) * scale
        square = turned * turned

        @pl.when(s == 0)
        def _():
            acc[h] = square

        @pl.when(s > 0)
        def _():
            acc[h] = acc[h] + square

        @pl.when(s == seqs - 1)
        def _():
            start = pl.multiple_of(h * PIECE, PIECE)
            for i in range(PIECE // 128):
                result[pl.ds(start + i * 128, 128), :] = acc[h, :, i * 128:(i + 1) * 128].T
            out_copy(h).start()

    def drain(j):
        arrived(g_all.at[j, c, pl.ds(0, Z - 1)], r_send.at[j])
        across(j).wait_send()
        far_copy(j).wait_send()
        behind_copy(j).wait_send()
        ahead_copy(j).wait_send()

        @pl.when(moves)
        def _():
            arrived(g_all.at[j, c, 0], w_send.at[j])
            f_copy(j).wait_send()

    def prepare():
        arrived(act_flat, b_sem.at[0])
        arrived(grad_flat, b_sem.at[1])
        high, low = spread(act_flat[...].reshape(64, half // 8), 0, half)
        high, low = high.T, low.T
        for i, part in enumerate((high, high, low)):
            act_diag[:, i * half:(i + 1) * half] = part

        @pl.loop(0, pieces)
        def _(i):
            grad_diag[i, :PIECE], grad_diag[i, PIECE:] = spread(grad_flat[...].reshape(64, units // 8), i, PIECE)

    @pl.loop(0, stages)
    def _(j):
        @pl.when(stays)
        def _():
            local(grads_view(j), g_all.at[j, c, z], g_recv.at[j, z]).start()

        @pl.when(moves)
        def _():
            remote(grads_view(j), g_all.at[j, xh, z], w_send.at[j], g_recv.at[j, z], swapped).start()

    for s in range(seqs):
        local(a2a_view(s, z), a2.at[s, z], a_recv.at[s, z]).start()
    for d in (4, 3, 2, 1):
        a2a(0, d)

    def when_stage(j, step):
        @pl.when(jnp.logical_and(j >= 0, j < stages))
        def _():
            step(j)

    events = {
        1: (prepare,), 2: (lambda: xsend(0), lambda: a2a(1, 4)), 3: (lambda: a2a(1, 3),), 4: (lambda: a2a(1, 2), lambda: xpass(0)), 5: (lambda: a2a(1, 1),),
        6: (lambda: a2a(2, 4),), 7: (lambda: a2a(2, 3),), 8: (lambda: xsend(1), lambda: a2a(2, 2)), 9: (lambda: a2a(2, 1),), 10: (lambda: xpass(1),),
        12: (lambda: xsend(2),), 14: (lambda: xpass(2),),
    }

    @pl.loop(0, stages + 20)
    def _(tick):
        for k in (4, 3, 2, 1, 0):
            when_stage(tick - 2 * k, functools.partial(hop, k=k))
        for t, calls in events.items():
            @pl.when(tick == t)
            def _():
                for call in calls:
                    call()
        when_stage(tick - 9, multiply)
        when_stage(tick - 11, relay)
        when_stage(tick - 13, reduce)
        when_stage(tick - 16, finish)
        when_stage(tick - 19, drain)

    @pl.loop(0, seqs)
    def _(s):
        arrived(a2.at[s, pl.ds(0, Z - 1)], a_send.at[s])
        arrived(a_all.at[s, pl.ds(0, len(direct))], x_send.at[s])
        for i in range(len(passing)):
            pass_copy(s, i).wait_send()

    @pl.loop(0, pieces)
    def _(h):
        out_copy(h).wait()


def shards(acts, grads, act_basis, grad_basis):
    seqs, rows, inputs = acts.shape
    units = grads.shape[2]
    width = inputs // (Y * Z)
    half = width // 2
    pieces = units // PIECE
    stages = seqs * pieces
    length = rows * Y * Z * 2
    dma = pltpu.SemaphoreType.DMA
    return pl.pallas_call(
        functools.partial(kernel, scale=length ** -0.5),
        out_shape=jax.ShapeDtypeStruct((units, half), F32),
        in_specs=[pl.BlockSpec(memory_space=pl.ANY)] * 4,
        out_specs=pl.BlockSpec(memory_space=pl.ANY),
        scratch_shapes=[
            pltpu.VMEM((seqs, Z, rows, width), BF16),
            pltpu.VMEM((seqs, 2 * Y, Z, rows, half), BF16),
            pltpu.VMEM((Y * half, 2 * Z * rows), BF16),
            pltpu.VMEM((stages, 2, Z, rows, PIECE), BF16),
            pltpu.VMEM((stages, 3, half, PIECE), BF16),
            pltpu.VMEM((stages, half, PIECE), BF16),
            pltpu.VMEM((stages, 2, half, PIECE), BF16),
            pltpu.VMEM((stages, half, PIECE), F32),
            pltpu.VMEM((stages, half, PIECE), F32),
            pltpu.VMEM((stages, half, PIECE), BF16),
            pltpu.VMEM((stages, half, PIECE), BF16),
            pltpu.VMEM((pieces, half, PIECE), F32),
            pltpu.VMEM((units, half), F32),
            pltpu.VMEM((8, 8, half // 8), F32),
            pltpu.VMEM((8, 8, units // 8), F32),
            pltpu.VMEM((half, 3 * half), BF16),
            pltpu.VMEM((pieces, 2 * PIECE, PIECE), BF16),
            dma((seqs,)), dma((seqs, Z)), dma((stages,)),
            dma((stages,)), dma((stages, Z)),
            dma((stages,)), dma((stages,)),
            dma((seqs,)), dma((seqs, 2 * Y)), dma((seqs, 2)),
            dma((stages,)), dma((stages,)), dma((stages, 2)), dma((stages, 2)),
            dma((stages,)), dma((stages,)), dma((2,)), dma((pieces,)),
        ],
        compiler_params=pltpu.CompilerParams(
            collective_id=0, has_side_effects=True, vmem_limit_bytes=56 << 20
        ),
        name="gathered",
    )(acts, grads, act_basis.transpose(1, 2, 0), grad_basis.transpose(1, 2, 0))


def solution(mesh):
    placed = (
        P(None, "tok", None),
        P(None, "tok", "out"),
        P("tok", None, None),
        P("out", None, None),
    )
    return jax.shard_map(
        shards, mesh=mesh, in_specs=placed, out_specs=P("out", "tok"), check_vma=False
    )
```

```python
import functools

import jax
import jax.numpy as jnp
from jax import lax
from jax.experimental import pallas as pl
from jax.experimental.pallas import tpu as pltpu
from jax.sharding import PartitionSpec as P

MESH = pl.DeviceIdType.MESH
Y, Z, X = 4, 8, 4
PIECE = 256
BF16, F32 = jnp.bfloat16, jnp.float32


def halves(v):
    high = v.astype(BF16)
    return high, (v - high.astype(F32)).astype(BF16)


def dot(a, b):
    return jnp.dot(a, b, preferred_element_type=F32)


def over(a, n):
    return jnp.right_shift(a, n.bit_length() - 1)


def mod(a, n):
    return jnp.bitwise_and(a, n - 1)


def iota(shape, dim):
    return lax.broadcasted_iota(jnp.int32, shape, dim)


def spread(flat, j, size):
    blocks = flat.shape[1]
    first = j * (size // 8)
    repeat = (iota((size, blocks), 1) == first + lax.div(iota((size, blocks), 0), 8)).astype(BF16)
    mine = lax.div(iota((size, 64), 1), 8) == lax.rem(iota((size, 64), 0), 8)
    fold = (lax.rem(iota((64, size), 1), 8) == lax.rem(iota((64, size), 0), 8)).astype(BF16)
    diagonal = lax.div(iota((size, size), 0), 8) == lax.div(iota((size, size), 1), 8)
    parts = []
    for part in halves(flat):
        rows = lax.dot_general(repeat, part, (((1,), (1,)), ((), ())), preferred_element_type=F32)
        rows = jnp.where(mine, rows, 0.0).astype(BF16)
        parts.append(jnp.where(diagonal, dot(rows, fold), 0.0).astype(BF16))
    return parts


def kernel(
    acts, grads, act_basis, grad_basis, out,
    a2, a_all, a_t, g_all, snd, rly, rcv, nxt, own, fin, landed, acc, result, act_flat, grad_flat, act_diag, grad_diag,
    a_send, a_recv, w_send, r_send, g_recv, k_send, k_recv,
    x_send, x_recv, v_send, q_send, q_recv, y_send, y_recv, f_send, f_recv, b_sem, o_sem,
    *, scale,
):
    seqs, rows, _ = acts.shape
    units = grads.shape[2]
    pieces = units // PIECE
    stages = seqs * pieces
    width = a2.shape[-1]
    half = width // 2
    depth = 2 * Z * rows
    tok, place = lax.axis_index("tok"), lax.axis_index("out")
    xh, z, y = mod(tok, 2), mod(over(tok, 2), Z), over(tok, 2 * Z)
    c, xl = mod(place, 2), over(place, 2)
    x = 2 * xh + xl
    sgn = 1 - 2 * c
    chunk = 2 * xl + c

    def dev(xi, yi, zi, ci):
        return ((yi * Z + zi) * 2 + over(xi, 2), 2 * mod(xi, 2) + ci)

    swapped = ((y * Z + z) * 2 + c, 2 * xl + xh)
    stays = xh == c
    moves = jnp.logical_not(stays)

    def remote(src, dst, send, recv, device):
        return pltpu.make_async_remote_copy(
            src_ref=src, dst_ref=dst, send_sem=send, recv_sem=recv,
            device_id=device, device_id_type=MESH,
        )

    def local(src, dst, sem):
        return pltpu.make_async_copy(src, dst, sem)

    def arrived(ref, sem):
        local(ref, ref, sem).wait()

    local(act_basis, act_flat, b_sem.at[0]).start()
    local(grad_basis, grad_flat, b_sem.at[1]).start()
    barrier = pltpu.get_barrier_semaphore()

    def greet(device):
        pl.semaphore_signal(barrier, inc=1, device_id=device, device_id_type=MESH)

    @pl.loop(1, Z)
    def _(d):
        greet(dev(x, y, mod(z + d, Z), c))

    @pl.loop(1, Y)
    def _(d):
        greet(dev(x, mod(y + d, Y), z, c))

    @pl.loop(1, 2 * X)
    def _(d):
        greet(dev(mod(x + over(d, 2), X), y, z, mod(c + d, 2)))

    pl.semaphore_wait(barrier, (Z - 1) + (Y - 1) + (2 * X - 1))

    def a2a_view(s, zt):
        return acts.at[s, :, pl.ds(pl.multiple_of((chunk * Z + zt) * width, width), width)]

    def a2a(s, d):
        for step in {d, Z - d}:
            zt = mod(z + step, Z)
            remote(a2a_view(s, zt), a2.at[s, z], a_send.at[s], a_recv.at[s, z], dev(x, y, zt, c)).start()

    def grads_view(j):
        s, h = over(j, pieces), mod(j, pieces)
        return grads.at[s, :, pl.ds(pl.multiple_of(h * PIECE, PIECE), PIECE)]

    def block(k):
        return mod(z + k * sgn, Z)

    forth, back, partner = dev(x, y, mod(z + sgn, Z), c), dev(x, y, mod(z - sgn, Z), c), dev(x, y, z, 1 - c)

    def ring(j, zz, to, sem):
        return remote(g_all.at[j, c, zz], g_all.at[j, c, zz], sem, g_recv.at[j, zz], to)

    def long(j, k):
        return ring(j, block(-k), forth, r_send.at[j])

    def short(j, k):
        return ring(j, block(k), back, r_send.at[j])

    def across(j):
        return remote(g_all.at[j, c], g_all.at[j, c], k_send.at[j], k_recv.at[j], partner)

    def hop(j, k):
        zz = block(-k)
        arrived(g_all.at[j, c, zz], g_recv.at[j, zz])
        long(j, k).start()
        if k > 0:
            zz = block(k)
            arrived(g_all.at[j, c, zz], g_recv.at[j, zz])
        if k < 3:
            short(j, k).start()

    def last_hop(j):
        zz = block(-4)
        arrived(g_all.at[j, c, zz], g_recv.at[j, zz])
        across(j).start()

    def x_copy(s, d):
        h = mod(c + d, 2)
        cols = pl.ds(pl.multiple_of(h * half, half), half)
        return remote(a2.at[s, :, :, cols], a_all.at[s, 2 * chunk + xh], x_send.at[s],
                      x_recv.at[s, 2 * chunk + xh], dev(mod(x + over(d, 2), X), y, z, h))

    direct = 5

    def xsend(s):
        @pl.loop(0, Z)
        def _(zz):
            arrived(a2.at[s, zz], a_recv.at[s, zz])

        for d in (2, 3, 6, 7):
            x_copy(s, mod(d + 4 * c, 2 * X)).start()
        x_copy(s, 1).start()

        cols = pl.ds(pl.multiple_of(c * half, half), half)
        local(a2.at[s, :, :, cols], a_all.at[s, 2 * chunk + xh], x_recv.at[s, 2 * chunk + xh]).start()

    def slot(dx, ci):
        xi = mod(x + dx, X)
        return 2 * (2 * mod(xi, 2) + ci) + over(xi, 2)

    passing = ((X - 1, 0, 1), (1, 1, X - 1))

    def pass_copy(s, i):
        dx, ci, to = passing[i]
        u = slot(dx, ci)
        return remote(a_all.at[s, u], a_all.at[s, u], v_send.at[s, i], x_recv.at[s, u],
                      dev(mod(x + to, X), y, z, c))

    def xpass(s):
        for i, (dx, ci, to) in enumerate(passing):
            u = slot(dx, ci)
            arrived(a_all.at[s, u], x_recv.at[s, u])
            pass_copy(s, i).start()

    def xrest(s):
        for dx in range(X):
            for ci in range(2):
                if (dx, ci) in ((X - 1, 0), (1, 1)):
                    continue
                u = slot(dx, ci)
                arrived(a_all.at[s, u], x_recv.at[s, u])
        for i, yi in enumerate((far, behind, ahead, y)):
            a_t[s % 2, i * half:(i + 1) * half, :] = a_all[s, pl.ds(2 * yi, 2)].reshape(depth, half).T

    ahead, behind, far = mod(y + sgn, Y), mod(y - sgn, Y), mod(y + 2, Y)
    up, down = dev(x, ahead, z, c), dev(x, behind, z, c)

    def far_copy(j):
        return remote(snd.at[j, 0], rly.at[j], q_send.at[j], q_recv.at[j], up)

    def behind_copy(j):
        return remote(snd.at[j, 1], rcv.at[j, 0], y_send.at[j, 0], y_recv.at[j, 0], down)

    def ahead_copy(j):
        return remote(snd.at[j, 2], rcv.at[j, 1], y_send.at[j, 1], y_recv.at[j, 1], up)

    def multiply(j):
        if j % pieces == 0:
            xrest(j // pieces)

        arrived(g_all.at[j, 1 - c], k_recv.at[j])
        product = dot(a_t[j // pieces % 2], g_all[j].reshape(depth, PIECE))
        snd[j, 0] = product[:half].astype(BF16)
        snd[j, 1] = product[half:2 * half].astype(BF16)
        nxt[j] = product[2 * half:3 * half]
        own[j] = product[3 * half:]
        far_copy(j).start()
        behind_copy(j).start()

    def relay(j):
        arrived(rly.at[j], q_recv.at[j])
        snd[j, 2] = (nxt[j] + rly[j].astype(F32)).astype(BF16)
        ahead_copy(j).start()

    def f_copy(j):
        return remote(fin.at[j], landed.at[j], f_send.at[j], f_recv.at[j], swapped)

    def reduce(j):
        for i in range(2):
            arrived(rcv.at[j, i], y_recv.at[j, i])
        total = own[j] + (rcv[j, 0].astype(F32) + rcv[j, 1].astype(F32))
        fin[j] = total.astype(BF16)

        @pl.when(stays)
        def _():
            local(fin.at[j], landed.at[j], f_recv.at[j]).start()

        @pl.when(moves)
        def _():
            f_copy(j).start()

    def out_copy(h):
        view = pl.ds(h * PIECE, PIECE)
        return local(result.at[view], out.at[view], o_sem.at[h])

    def finish(j):
        s, h = divmod(j, pieces)
        arrived(landed.at[j], f_recv.at[j])
        piece = landed[j]
        high, low = halves(dot(jnp.concatenate([piece, piece], axis=1), grad_diag[h]))
        turned = dot(act_diag[...], jnp.concatenate([high, low, high], axis=0)) * scale
        square = turned * turned
        if s > 0:
            square = acc[h] + square
        if s < seqs - 1:
            acc[h] = square
        else:
            result[h * PIECE:(h + 1) * PIECE, :] = square.T
            out_copy(h).start()

    def drain(j):
        arrived(g_all.at[j, c, pl.ds(0, Z - 1)], r_send.at[j])
        across(j).wait_send()
        far_copy(j).wait_send()
        behind_copy(j).wait_send()
        ahead_copy(j).wait_send()

        @pl.when(moves)
        def _():
            arrived(g_all.at[j, c, 0], w_send.at[j])
            f_copy(j).wait_send()

    def prepare():
        arrived(act_flat, b_sem.at[0])
        arrived(grad_flat, b_sem.at[1])
        high, low = spread(act_flat[...].reshape(64, half // 8), 0, half)
        high, low = high.T, low.T
        for i, part in enumerate((high, high, low)):
            act_diag[:, i * half:(i + 1) * half] = part

        @pl.loop(0, pieces)
        def _(i):
            grad_diag[i, :PIECE], grad_diag[i, PIECE:] = spread(grad_flat[...].reshape(64, units // 8), i, PIECE)

    @pl.loop(0, stages)
    def _(j):
        @pl.when(stays)
        def _():
            local(grads_view(j), g_all.at[j, c, z], g_recv.at[j, z]).start()

        @pl.when(moves)
        def _():
            remote(grads_view(j), g_all.at[j, xh, z], w_send.at[j], g_recv.at[j, z], swapped).start()

    for s in range(seqs):
        local(a2a_view(s, z), a2.at[s, z], a_recv.at[s, z]).start()
    for d in (4, 3, 2, 1):
        a2a(0, d)

    plan = []

    def put(at, step, *args):
        plan.append((at, len(plan), step, args))

    put(0.9, prepare)
    for s, sends, go, through in ((0, (), 0.99, 3.1), (1, (3.3, 3.8, 4.3, 4.7), 6.45, 8.1), (2, (5.1, 5.6, 6.1, 6.5), 8.5, 11.1)):
        for at, d in zip(sends, (4, 3, 2, 1)):
            put(at, a2a, s, d)
        put(go, xsend, s)
        put(through, xpass, s)
    for j in range(stages):
        first = j < pieces
        for k in range(4):
            put(k + j / pieces if first else j - pieces + 1 + 2 * k + (4 - k) / 10, hop, j, k)
        put(4 + j / 10 if first else j + 5, last_hop, j)
        put(4.6 + 0.3 * j if first else j + 5.9, multiply, j)
        put(6.2 + 0.3 * j if first else j + 7.92, relay, j)
        put(8.7 + 0.5 * j if first else j + 10.1, reduce, j)
        put(max(j + 13.2, 17.2 + j / 2), finish, j)
        put(j + 14.5, drain, j)

    for _, _, step, args in sorted(plan, key=lambda call: call[:2]):
        step(*args)

    @pl.loop(0, seqs)
    def _(s):
        arrived(a2.at[s, pl.ds(0, Z - 1)], a_send.at[s])
        arrived(a_all.at[s, pl.ds(0, direct)], x_send.at[s])
        for i in range(len(passing)):
            pass_copy(s, i).wait_send()

    for h in range(pieces):
        out_copy(h).wait()


def shards(acts, grads, act_basis, grad_basis):
    seqs, rows, inputs = acts.shape
    units = grads.shape[2]
    width = inputs // (Y * Z)
    half = width // 2
    pieces = units // PIECE
    stages = seqs * pieces
    length = rows * Y * Z * 2
    dma = pltpu.SemaphoreType.DMA
    return pl.pallas_call(
        functools.partial(kernel, scale=length ** -0.5),
        out_shape=jax.ShapeDtypeStruct((units, half), F32),
        in_specs=[pl.BlockSpec(memory_space=pl.ANY)] * 4,
        out_specs=pl.BlockSpec(memory_space=pl.ANY),
        scratch_shapes=[
            pltpu.VMEM((seqs, Z, rows, width), BF16),
            pltpu.VMEM((seqs, 2 * Y, Z, rows, half), BF16),
            pltpu.VMEM((2, Y * half, 2 * Z * rows), BF16),
            pltpu.VMEM((stages, 2, Z, rows, PIECE), BF16),
            pltpu.VMEM((stages, 3, half, PIECE), BF16),
            pltpu.VMEM((stages, half, PIECE), BF16),
            pltpu.VMEM((stages, 2, half, PIECE), BF16),
            pltpu.VMEM((stages, half, PIECE), F32),
            pltpu.VMEM((stages, half, PIECE), F32),
            pltpu.VMEM((stages, half, PIECE), BF16),
            pltpu.VMEM((stages, half, PIECE), BF16),
            pltpu.VMEM((pieces, half, PIECE), F32),
            pltpu.VMEM((units, half), F32),
            pltpu.VMEM((8, 8, half // 8), F32),
            pltpu.VMEM((8, 8, units // 8), F32),
            pltpu.VMEM((half, 3 * half), BF16),
            pltpu.VMEM((pieces, 2 * PIECE, PIECE), BF16),
            dma((seqs,)), dma((seqs, Z)), dma((stages,)),
            dma((stages,)), dma((stages, Z)),
            dma((stages,)), dma((stages,)),
            dma((seqs,)), dma((seqs, 2 * Y)), dma((seqs, 2)),
            dma((stages,)), dma((stages,)), dma((stages, 2)), dma((stages, 2)),
            dma((stages,)), dma((stages,)), dma((2,)), dma((pieces,)),
        ],
        compiler_params=pltpu.CompilerParams(
            collective_id=0, has_side_effects=True, vmem_limit_bytes=56 << 20
        ),
        name="gathered",
    )(acts, grads, act_basis.transpose(1, 2, 0), grad_basis.transpose(1, 2, 0))


def solution(mesh):
    placed = (
        P(None, "tok", None),
        P(None, "tok", "out"),
        P("tok", None, None),
        P("out", None, None),
    )
    return jax.shard_map(
        shards, mesh=mesh, in_specs=placed, out_specs=P("out", "tok"), check_vma=False
    )
```

```python
import functools

import jax
import jax.numpy as jnp
from jax import lax
from jax.experimental import pallas as pl
from jax.experimental.pallas import tpu as pltpu
from jax.sharding import PartitionSpec as P

MESH = pl.DeviceIdType.MESH
Y, Z, X = 4, 8, 4
PIECE = 256
BF16, F32 = jnp.bfloat16, jnp.float32


def halves(v):
    high = v.astype(BF16)
    return high, (v - high.astype(F32)).astype(BF16)


def dot(a, b):
    return jnp.dot(a, b, preferred_element_type=F32)


def over(a, n):
    return jnp.right_shift(a, n.bit_length() - 1)


def mod(a, n):
    return jnp.bitwise_and(a, n - 1)


def iota(shape, dim):
    return lax.broadcasted_iota(jnp.int32, shape, dim)


def spread(flat, j, size):
    blocks = flat.shape[1]
    first = j * (size // 8)
    repeat = (iota((size, blocks), 1) == first + lax.div(iota((size, blocks), 0), 8)).astype(BF16)
    mine = lax.div(iota((size, 64), 1), 8) == lax.rem(iota((size, 64), 0), 8)
    fold = (lax.rem(iota((64, size), 1), 8) == lax.rem(iota((64, size), 0), 8)).astype(BF16)
    diagonal = lax.div(iota((size, size), 0), 8) == lax.div(iota((size, size), 1), 8)
    parts = []
    for part in halves(flat):
        rows = lax.dot_general(repeat, part, (((1,), (1,)), ((), ())), preferred_element_type=F32)
        rows = jnp.where(mine, rows, 0.0).astype(BF16)
        parts.append(jnp.where(diagonal, dot(rows, fold), 0.0).astype(BF16))
    return parts


def kernel(
    acts, grads, act_basis, grad_basis, out,
    a2, a_all, a_t, g_all, snd, rly, rcv, nxt, own, fin, landed, acc, result, act_flat, grad_flat, act_diag, grad_diag,
    a_send, a_recv, w_send, r_send, g_recv, k_send, k_recv,
    x_send, x_recv, v_send, q_send, q_recv, y_send, y_recv, f_send, f_recv, b_sem, o_sem,
    *, scale,
):
    seqs, rows, _ = acts.shape
    units = grads.shape[2]
    pieces = units // PIECE
    stages = seqs * pieces
    width = a2.shape[-1]
    half = width // 2
    depth = 2 * Z * rows
    tok, place = lax.axis_index("tok"), lax.axis_index("out")
    xh, z, y = mod(tok, 2), mod(over(tok, 2), Z), over(tok, 2 * Z)
    c, xl = mod(place, 2), over(place, 2)
    x = 2 * xh + xl
    sgn = 1 - 2 * c
    chunk = 2 * xl + c

    def dev(xi, yi, zi, ci):
        return ((yi * Z + zi) * 2 + over(xi, 2), 2 * mod(xi, 2) + ci)

    swapped = ((y * Z + z) * 2 + c, 2 * xl + xh)
    stays = xh == c
    moves = jnp.logical_not(stays)

    def remote(src, dst, send, recv, device):
        return pltpu.make_async_remote_copy(
            src_ref=src, dst_ref=dst, send_sem=send, recv_sem=recv,
            device_id=device, device_id_type=MESH,
        )

    def local(src, dst, sem):
        return pltpu.make_async_copy(src, dst, sem)

    def arrived(ref, sem):
        local(ref, ref, sem).wait()

    local(act_basis, act_flat, b_sem.at[0]).start()
    local(grad_basis, grad_flat, b_sem.at[1]).start()
    barrier = pltpu.get_barrier_semaphore()

    def greet(device):
        pl.semaphore_signal(barrier, inc=1, device_id=device, device_id_type=MESH)

    @pl.loop(1, Z)
    def _(d):
        greet(dev(x, y, mod(z + d, Z), c))

    @pl.loop(1, Y)
    def _(d):
        greet(dev(x, mod(y + d, Y), z, c))

    @pl.loop(1, 2 * X)
    def _(d):
        greet(dev(mod(x + over(d, 2), X), y, z, mod(c + d, 2)))

    pl.semaphore_wait(barrier, (Z - 1) + (Y - 1) + (2 * X - 1))

    def a2a_view(s, zt):
        return acts.at[s, :, pl.ds(pl.multiple_of((chunk * Z + zt) * width, width), width)]

    def a2a(s, d):
        for step in {d, Z - d}:
            zt = mod(z + step, Z)
            remote(a2a_view(s, zt), a2.at[s, z], a_send.at[s], a_recv.at[s, z], dev(x, y, zt, c)).start()

    def grads_view(j):
        s, h = over(j, pieces), mod(j, pieces)
        return grads.at[s, :, pl.ds(pl.multiple_of(h * PIECE, PIECE), PIECE)]

    def block(k):
        return mod(z + k * sgn, Z)

    forth, back, partner = dev(x, y, mod(z + sgn, Z), c), dev(x, y, mod(z - sgn, Z), c), dev(x, y, z, 1 - c)

    def ring(j, zz, to, sem):
        return remote(g_all.at[j, c, zz], g_all.at[j, c, zz], sem, g_recv.at[j, zz], to)

    def long(j, k):
        return ring(j, block(-k), forth, r_send.at[j])

    def short(j, k):
        return ring(j, block(k), back, r_send.at[j])

    def across(j):
        return remote(g_all.at[j, c], g_all.at[j, c], k_send.at[j], k_recv.at[j], partner)

    def hop(j, k):
        zz = block(-k)
        arrived(g_all.at[j, c, zz], g_recv.at[j, zz])
        long(j, k).start()
        if k > 0:
            zz = block(k)
            arrived(g_all.at[j, c, zz], g_recv.at[j, zz])
        if k < 3:
            short(j, k).start()

    def last_hop(j):
        zz = block(-4)
        arrived(g_all.at[j, c, zz], g_recv.at[j, zz])
        across(j).start()

    def x_copy(s, d):
        h = mod(c + d, 2)
        cols = pl.ds(pl.multiple_of(h * half, half), half)
        return remote(a2.at[s, :, :, cols], a_all.at[s, 2 * chunk + xh], x_send.at[s],
                      x_recv.at[s, 2 * chunk + xh], dev(mod(x + over(d, 2), X), y, z, h))

    direct = 5

    def xsend(s):
        @pl.loop(0, Z)
        def _(zz):
            arrived(a2.at[s, zz], a_recv.at[s, zz])

        for d in (2, 3, 6, 7):
            x_copy(s, mod(d + 4 * c, 2 * X)).start()
        x_copy(s, 1).start()

        cols = pl.ds(pl.multiple_of(c * half, half), half)
        local(a2.at[s, :, :, cols], a_all.at[s, 2 * chunk + xh], x_recv.at[s, 2 * chunk + xh]).start()

    def slot(dx, ci):
        xi = mod(x + dx, X)
        return 2 * (2 * mod(xi, 2) + ci) + over(xi, 2)

    passing = ((X - 1, 0, 1), (1, 1, X - 1))

    def pass_copy(s, i):
        dx, ci, to = passing[i]
        u = slot(dx, ci)
        return remote(a_all.at[s, u], a_all.at[s, u], v_send.at[s, i], x_recv.at[s, u],
                      dev(mod(x + to, X), y, z, c))

    def xpass(s):
        for i, (dx, ci, to) in enumerate(passing):
            u = slot(dx, ci)
            arrived(a_all.at[s, u], x_recv.at[s, u])
            pass_copy(s, i).start()

    def xrest(s):
        for dx in range(X):
            for ci in range(2):
                if (dx, ci) in ((X - 1, 0), (1, 1)):
                    continue
                u = slot(dx, ci)
                arrived(a_all.at[s, u], x_recv.at[s, u])
        for i, yi in enumerate((far, behind, ahead, y)):
            a_t[s % 2, i * half:(i + 1) * half, :] = a_all[s, pl.ds(2 * yi, 2)].reshape(depth, half).T

    ahead, behind, far = mod(y + sgn, Y), mod(y - sgn, Y), mod(y + 2, Y)
    up, down = dev(x, ahead, z, c), dev(x, behind, z, c)

    def far_copy(j):
        return remote(snd.at[j, 0], rly.at[j], q_send.at[j], q_recv.at[j], up)

    def behind_copy(j):
        return remote(snd.at[j, 1], rcv.at[j, 0], y_send.at[j, 0], y_recv.at[j, 0], down)

    def ahead_copy(j):
        return remote(snd.at[j, 2], rcv.at[j, 1], y_send.at[j, 1], y_recv.at[j, 1], up)

    def multiply(j):
        if j % pieces == 0:
            xrest(j // pieces)

        arrived(g_all.at[j, 1 - c], k_recv.at[j])
        product = dot(a_t[j // pieces % 2], g_all[j].reshape(depth, PIECE))
        snd[j, 0] = product[:half].astype(BF16)
        snd[j, 1] = product[half:2 * half].astype(BF16)
        nxt[j] = product[2 * half:3 * half]
        own[j] = product[3 * half:]
        far_copy(j).start()
        behind_copy(j).start()

    def relay(j):
        arrived(rly.at[j], q_recv.at[j])
        snd[j, 2] = (nxt[j] + rly[j].astype(F32)).astype(BF16)
        ahead_copy(j).start()

    def f_copy(j):
        return remote(fin.at[j], landed.at[j], f_send.at[j], f_recv.at[j], swapped)

    def reduce(j):
        for i in range(2):
            arrived(rcv.at[j, i], y_recv.at[j, i])
        total = own[j] + (rcv[j, 0].astype(F32) + rcv[j, 1].astype(F32))
        fin[j] = total.astype(BF16)

        @pl.when(stays)
        def _():
            local(fin.at[j], landed.at[j], f_recv.at[j]).start()

        @pl.when(moves)
        def _():
            f_copy(j).start()

    def out_copy(h):
        view = pl.ds(h * PIECE, PIECE)
        return local(result.at[view], out.at[view], o_sem.at[h])

    def finish(j):
        s, h = divmod(j, pieces)
        arrived(landed.at[j], f_recv.at[j])
        piece = landed[j]
        high, low = halves(dot(jnp.concatenate([piece, piece], axis=1), grad_diag[h]))
        turned = dot(act_diag[...], jnp.concatenate([high, low, high], axis=0)) * scale
        square = turned * turned
        if s > 0:
            square = acc[h] + square
        if s < seqs - 1:
            acc[h] = square
        else:
            result[h * PIECE:(h + 1) * PIECE, :] = square.T
            out_copy(h).start()

    def drain(j):
        arrived(g_all.at[j, c, pl.ds(0, Z - 1)], r_send.at[j])
        across(j).wait_send()
        far_copy(j).wait_send()
        behind_copy(j).wait_send()
        ahead_copy(j).wait_send()

        @pl.when(moves)
        def _():
            arrived(g_all.at[j, c, 0], w_send.at[j])
            f_copy(j).wait_send()

    def prepare():
        arrived(act_flat, b_sem.at[0])
        arrived(grad_flat, b_sem.at[1])
        high, low = spread(act_flat[...].reshape(64, half // 8), 0, half)
        high, low = high.T, low.T
        for i, part in enumerate((high, high, low)):
            act_diag[:, i * half:(i + 1) * half] = part

        @pl.loop(0, pieces)
        def _(i):
            grad_diag[i, :PIECE], grad_diag[i, PIECE:] = spread(grad_flat[...].reshape(64, units // 8), i, PIECE)

    @pl.loop(0, stages)
    def _(j):
        @pl.when(stays)
        def _():
            local(grads_view(j), g_all.at[j, c, z], g_recv.at[j, z]).start()

        @pl.when(moves)
        def _():
            remote(grads_view(j), g_all.at[j, xh, z], w_send.at[j], g_recv.at[j, z], swapped).start()

    for s in range(seqs):
        local(a2a_view(s, z), a2.at[s, z], a_recv.at[s, z]).start()
    for d in (4, 3, 2, 1):
        a2a(0, d)

    plan = []

    def put(at, step, *args):
        plan.append((at, len(plan), step, args))

    put(0.9, prepare)
    for s, sends, go, through in ((0, (), 0.99, 3.1), (1, (2.9, 3.4, 3.9, 4.35), 5.7, 8.45), (2, (5.1, 5.6, 6.0, 6.35), 8.15, 11.3)):
        for at, d in zip(sends, (4, 3, 2, 1)):
            put(at, a2a, s, d)
        put(go, xsend, s)
        put(through, xpass, s)
    for j in range(stages):
        first = j < pieces
        for k in range(4):
            put(k + j / pieces if first else j - pieces + 1 + 2 * k + (4 - k) / 10, hop, j, k)
        put(4 + j / 10 if first else j + 5, last_hop, j)
        put(4.6 + 0.3 * j if first else j + 5.9, multiply, j)
        put(6.95 + 0.35 * j if first else j + 7.92, relay, j)
        put(8.7 + 0.5 * j if first else j + 10.1, reduce, j)
        put(max(j + 13.2, 17.2 + j / 2), finish, j)
        put(j + 14.5, drain, j)

    for _, _, step, args in sorted(plan, key=lambda call: call[:2]):
        step(*args)

    @pl.loop(0, seqs)
    def _(s):
        arrived(a2.at[s, pl.ds(0, Z - 1)], a_send.at[s])
        arrived(a_all.at[s, pl.ds(0, direct)], x_send.at[s])
        for i in range(len(passing)):
            pass_copy(s, i).wait_send()

    for h in range(pieces):
        out_copy(h).wait()


def shards(acts, grads, act_basis, grad_basis):
    seqs, rows, inputs = acts.shape
    units = grads.shape[2]
    width = inputs // (Y * Z)
    half = width // 2
    pieces = units // PIECE
    stages = seqs * pieces
    length = rows * Y * Z * 2
    dma = pltpu.SemaphoreType.DMA
    return pl.pallas_call(
        functools.partial(kernel, scale=length ** -0.5),
        out_shape=jax.ShapeDtypeStruct((units, half), F32),
        in_specs=[pl.BlockSpec(memory_space=pl.ANY)] * 4,
        out_specs=pl.BlockSpec(memory_space=pl.ANY),
        scratch_shapes=[
            pltpu.VMEM((seqs, Z, rows, width), BF16),
            pltpu.VMEM((seqs, 2 * Y, Z, rows, half), BF16),
            pltpu.VMEM((2, Y * half, 2 * Z * rows), BF16),
            pltpu.VMEM((stages, 2, Z, rows, PIECE), BF16),
            pltpu.VMEM((stages, 3, half, PIECE), BF16),
            pltpu.VMEM((stages, half, PIECE), BF16),
            pltpu.VMEM((stages, 2, half, PIECE), BF16),
            pltpu.VMEM((stages, half, PIECE), F32),
            pltpu.VMEM((stages, half, PIECE), F32),
            pltpu.VMEM((stages, half, PIECE), BF16),
            pltpu.VMEM((stages, half, PIECE), BF16),
            pltpu.VMEM((pieces, half, PIECE), F32),
            pltpu.VMEM((units, half), F32),
            pltpu.VMEM((8, 8, half // 8), F32),
            pltpu.VMEM((8, 8, units // 8), F32),
            pltpu.VMEM((half, 3 * half), BF16),
            pltpu.VMEM((pieces, 2 * PIECE, PIECE), BF16),
            dma((seqs,)), dma((seqs, Z)), dma((stages,)),
            dma((stages,)), dma((stages, Z)),
            dma((stages,)), dma((stages,)),
            dma((seqs,)), dma((seqs, 2 * Y)), dma((seqs, 2)),
            dma((stages,)), dma((stages,)), dma((stages, 2)), dma((stages, 2)),
            dma((stages,)), dma((stages,)), dma((2,)), dma((pieces,)),
        ],
        compiler_params=pltpu.CompilerParams(
            collective_id=0, has_side_effects=True, vmem_limit_bytes=56 << 20
        ),
        name="gathered",
    )(acts, grads, act_basis.transpose(1, 2, 0), grad_basis.transpose(1, 2, 0))


def solution(mesh):
    placed = (
        P(None, "tok", None),
        P(None, "tok", "out"),
        P("tok", None, None),
        P("out", None, None),
    )
    return jax.shard_map(
        shards, mesh=mesh, in_specs=placed, out_specs=P("out", "tok"), check_vma=False
    )
```

```python
import functools

import jax
import jax.numpy as jnp
from jax import lax
from jax.experimental import pallas as pl
from jax.experimental.pallas import tpu as pltpu
from jax.sharding import PartitionSpec as P

MESH = pl.DeviceIdType.MESH
Y, Z, X = 4, 8, 4
PIECE = 256
BF16, F32 = jnp.bfloat16, jnp.float32


def halves(v):
    high = v.astype(BF16)
    return high, (v - high.astype(F32)).astype(BF16)


def dot(a, b):
    return jnp.dot(a, b, preferred_element_type=F32)


def over(a, n):
    return jnp.right_shift(a, n.bit_length() - 1)


def mod(a, n):
    return jnp.bitwise_and(a, n - 1)


def iota(shape, dim):
    return lax.broadcasted_iota(jnp.int32, shape, dim)


def spread(flat, j, size):
    blocks = flat.shape[1]
    first = j * (size // 8)
    repeat = (iota((size, blocks), 1) == first + lax.div(iota((size, blocks), 0), 8)).astype(BF16)
    mine = lax.div(iota((size, 64), 1), 8) == lax.rem(iota((size, 64), 0), 8)
    fold = (lax.rem(iota((64, size), 1), 8) == lax.rem(iota((64, size), 0), 8)).astype(BF16)
    diagonal = lax.div(iota((size, size), 0), 8) == lax.div(iota((size, size), 1), 8)
    parts = []
    for part in halves(flat):
        rows = lax.dot_general(repeat, part, (((1,), (1,)), ((), ())), preferred_element_type=F32)
        rows = jnp.where(mine, rows, 0.0).astype(BF16)
        parts.append(jnp.where(diagonal, dot(rows, fold), 0.0).astype(BF16))
    return parts


def kernel(
    acts, grads, act_basis, grad_basis, out,
    a2, a_all, a_t, g_all, snd, rly, rcv, nxt, own, fin, landed, acc, result, act_flat, grad_flat, act_diag, grad_diag,
    a_send, a_recv, w_send, r_send, g_recv, k_send, k_recv,
    x_send, x_recv, v_send, q_send, q_recv, y_send, y_recv, f_send, f_recv, b_sem, o_sem,
    *, scale,
):
    seqs, rows, _ = acts.shape
    units = grads.shape[2]
    pieces = units // PIECE
    stages = seqs * pieces
    width = a2.shape[-1]
    half = width // 2
    depth = 2 * Z * rows
    tok, place = lax.axis_index("tok"), lax.axis_index("out")
    xh, z, y = mod(tok, 2), mod(over(tok, 2), Z), over(tok, 2 * Z)
    c, xl = mod(place, 2), over(place, 2)
    x = 2 * xh + xl
    sgn = 1 - 2 * c
    chunk = 2 * xl + c

    def dev(xi, yi, zi, ci):
        return ((yi * Z + zi) * 2 + over(xi, 2), 2 * mod(xi, 2) + ci)

    swapped = ((y * Z + z) * 2 + c, 2 * xl + xh)
    stays = xh == c
    moves = jnp.logical_not(stays)

    def remote(src, dst, send, recv, device):
        return pltpu.make_async_remote_copy(
            src_ref=src, dst_ref=dst, send_sem=send, recv_sem=recv,
            device_id=device, device_id_type=MESH,
        )

    def local(src, dst, sem):
        return pltpu.make_async_copy(src, dst, sem)

    def arrived(ref, sem):
        local(ref, ref, sem).wait()

    local(act_basis, act_flat, b_sem.at[0]).start()
    local(grad_basis, grad_flat, b_sem.at[1]).start()
    barrier = pltpu.get_barrier_semaphore()

    def greet(device):
        pl.semaphore_signal(barrier, inc=1, device_id=device, device_id_type=MESH)

    @pl.loop(1, Z)
    def _(d):
        greet(dev(x, y, mod(z + d, Z), c))

    @pl.loop(1, Y)
    def _(d):
        greet(dev(x, mod(y + d, Y), z, c))

    @pl.loop(1, 2 * X)
    def _(d):
        greet(dev(mod(x + over(d, 2), X), y, z, mod(c + d, 2)))

    pl.semaphore_wait(barrier, (Z - 1) + (Y - 1) + (2 * X - 1))

    def a2a_view(s, zt):
        return acts.at[s, :, pl.ds(pl.multiple_of((chunk * Z + zt) * width, width), width)]

    def a2a(s, d):
        for step in {d, Z - d}:
            zt = mod(z + step, Z)
            remote(a2a_view(s, zt), a2.at[s, z], a_send.at[s], a_recv.at[s, z], dev(x, y, zt, c)).start()

    def grads_view(j):
        s, h = over(j, pieces), mod(j, pieces)
        return grads.at[s, :, pl.ds(pl.multiple_of(h * PIECE, PIECE), PIECE)]

    def block(k):
        return mod(z + k * sgn, Z)

    forth, back, partner = dev(x, y, mod(z + sgn, Z), c), dev(x, y, mod(z - sgn, Z), c), dev(x, y, z, 1 - c)

    def ring(j, zz, to, sem):
        return remote(g_all.at[j, c, zz], g_all.at[j, c, zz], sem, g_recv.at[j, zz], to)

    def long(j, k):
        return ring(j, block(-k), forth, r_send.at[j])

    def short(j, k):
        return ring(j, block(k), back, r_send.at[j])

    def across(j):
        return remote(g_all.at[j, c], g_all.at[j, c], k_send.at[j], k_recv.at[j], partner)

    def hop(j, k):
        zz = block(-k)
        arrived(g_all.at[j, c, zz], g_recv.at[j, zz])
        long(j, k).start()
        if k > 0:
            zz = block(k)
            arrived(g_all.at[j, c, zz], g_recv.at[j, zz])
        if k < 3:
            short(j, k).start()

    def last_hop(j):
        zz = block(-4)
        arrived(g_all.at[j, c, zz], g_recv.at[j, zz])
        across(j).start()

    def x_copy(s, d):
        h = mod(c + d, 2)
        cols = pl.ds(pl.multiple_of(h * half, half), half)
        return remote(a2.at[s, :, :, cols], a_all.at[s, 2 * chunk + xh], x_send.at[s],
                      x_recv.at[s, 2 * chunk + xh], dev(mod(x + over(d, 2), X), y, z, h))

    direct = 5

    def xsend(s):
        @pl.loop(0, Z)
        def _(zz):
            arrived(a2.at[s, zz], a_recv.at[s, zz])

        for d in (2, 3, 6, 7):
            x_copy(s, mod(d + 4 * c, 2 * X)).start()
        x_copy(s, 1).start()

        cols = pl.ds(pl.multiple_of(c * half, half), half)
        local(a2.at[s, :, :, cols], a_all.at[s, 2 * chunk + xh], x_recv.at[s, 2 * chunk + xh]).start()

    def slot(dx, ci):
        xi = mod(x + dx, X)
        return 2 * (2 * mod(xi, 2) + ci) + over(xi, 2)

    passing = ((X - 1, 0, 1), (1, 1, X - 1))

    def pass_copy(s, i):
        dx, ci, to = passing[i]
        u = slot(dx, ci)
        return remote(a_all.at[s, u], a_all.at[s, u], v_send.at[s, i], x_recv.at[s, u],
                      dev(mod(x + to, X), y, z, c))

    def xpass(s):
        for i, (dx, ci, to) in enumerate(passing):
            u = slot(dx, ci)
            arrived(a_all.at[s, u], x_recv.at[s, u])
            pass_copy(s, i).start()

    def xrest(s):
        for dx in range(X):
            for ci in range(2):
                if (dx, ci) in ((X - 1, 0), (1, 1)):
                    continue
                u = slot(dx, ci)
                arrived(a_all.at[s, u], x_recv.at[s, u])
        for i, yi in enumerate((far, behind, ahead, y)):
            a_t[s % 2, i * half:(i + 1) * half, :] = a_all[s, pl.ds(2 * yi, 2)].reshape(depth, half).T

    ahead, behind, far = mod(y + sgn, Y), mod(y - sgn, Y), mod(y + 2, Y)
    up, down = dev(x, ahead, z, c), dev(x, behind, z, c)

    def far_copy(j):
        return remote(snd.at[j, 0], rly.at[j], q_send.at[j], q_recv.at[j], up)

    def behind_copy(j):
        return remote(snd.at[j, 1], rcv.at[j, 0], y_send.at[j, 0], y_recv.at[j, 0], down)

    def ahead_copy(j):
        return remote(snd.at[j, 2], rcv.at[j, 1], y_send.at[j, 1], y_recv.at[j, 1], up)

    def multiply(j):
        if j % pieces == 0:
            xrest(j // pieces)

        arrived(g_all.at[j, 1 - c], k_recv.at[j])
        product = dot(a_t[j // pieces % 2], g_all[j].reshape(depth, PIECE))
        snd[j, 0] = product[:half].astype(BF16)
        snd[j, 1] = product[half:2 * half].astype(BF16)
        nxt[j] = product[2 * half:3 * half]
        own[j] = product[3 * half:]
        far_copy(j).start()
        behind_copy(j).start()

    def relay(j):
        arrived(rly.at[j], q_recv.at[j])
        snd[j, 2] = (nxt[j] + rly[j].astype(F32)).astype(BF16)
        ahead_copy(j).start()

    def f_copy(j):
        return remote(fin.at[j], landed.at[j], f_send.at[j], f_recv.at[j], swapped)

    def reduce(j):
        for i in range(2):
            arrived(rcv.at[j, i], y_recv.at[j, i])
        total = own[j] + (rcv[j, 0].astype(F32) + rcv[j, 1].astype(F32))
        fin[j] = total.astype(BF16)

        @pl.when(stays)
        def _():
            local(fin.at[j], landed.at[j], f_recv.at[j]).start()

        @pl.when(moves)
        def _():
            f_copy(j).start()

    def out_copy(h):
        view = pl.ds(h * PIECE, PIECE)
        return local(result.at[view], out.at[view], o_sem.at[h])

    def finish(j):
        s, h = divmod(j, pieces)
        arrived(landed.at[j], f_recv.at[j])
        piece = landed[j]
        high, low = halves(dot(jnp.concatenate([piece, piece], axis=1), grad_diag[h]))
        turned = dot(act_diag[...], jnp.concatenate([high, low, high], axis=0)) * scale
        square = turned * turned
        if s > 0:
            square = acc[h] + square
        if s < seqs - 1:
            acc[h] = square
        else:
            result[h * PIECE:(h + 1) * PIECE, :] = square.T
            out_copy(h).start()

    def drain(j):
        arrived(g_all.at[j, c, pl.ds(0, Z - 1)], r_send.at[j])
        across(j).wait_send()
        far_copy(j).wait_send()
        behind_copy(j).wait_send()
        ahead_copy(j).wait_send()

        @pl.when(moves)
        def _():
            arrived(g_all.at[j, c, 0], w_send.at[j])
            f_copy(j).wait_send()

    def prepare():
        arrived(act_flat, b_sem.at[0])
        arrived(grad_flat, b_sem.at[1])
        high, low = spread(act_flat[...].reshape(64, half // 8), 0, half)
        high, low = high.T, low.T
        for i, part in enumerate((high, high, low)):
            act_diag[:, i * half:(i + 1) * half] = part

        @pl.loop(0, pieces)
        def _(i):
            grad_diag[i, :PIECE], grad_diag[i, PIECE:] = spread(grad_flat[...].reshape(64, units // 8), i, PIECE)

    @pl.loop(0, stages)
    def _(j):
        @pl.when(stays)
        def _():
            local(grads_view(j), g_all.at[j, c, z], g_recv.at[j, z]).start()

        @pl.when(moves)
        def _():
            remote(grads_view(j), g_all.at[j, xh, z], w_send.at[j], g_recv.at[j, z], swapped).start()

    for s in range(seqs):
        local(a2a_view(s, z), a2.at[s, z], a_recv.at[s, z]).start()
    for d in (4, 3, 2, 1):
        a2a(0, d)

    plan = []

    def put(at, step, *args):
        plan.append((at, len(plan), step, args))

    put(0.9, prepare)
    for s, sends, go, through in ((0, (), 0.99, 3.1), (1, (3.3, 3.8, 4.3, 4.7), 6.45, 8.45), (2, (5.1, 5.6, 6.1, 6.5), 8.35, 11.3)):
        for at, d in zip(sends, (4, 3, 2, 1)):
            put(at, a2a, s, d)
        put(go, xsend, s)
        put(through, xpass, s)
    for j in range(stages):
        first = j < pieces
        for k in range(4):
            put(k + j / pieces if first else j - pieces + 1 + 2 * k + (4 - k) / 10, hop, j, k)
        put(4 + j / 10 if first else j + 5, last_hop, j)
        put(4.6 + 0.3 * j if first else j + 5.9, multiply, j)
        put(6.2 + 0.3 * j if first else j + 7.92, relay, j)
        put(8.7 + 0.5 * j if first else j + 10.1, reduce, j)
        put(max(j + 13.2, 17.2 + j / 2), finish, j)
        put(j + 14.5, drain, j)

    for _, _, step, args in sorted(plan, key=lambda call: call[:2]):
        step(*args)

    @pl.loop(0, seqs)
    def _(s):
        arrived(a2.at[s, pl.ds(0, Z - 1)], a_send.at[s])
        arrived(a_all.at[s, pl.ds(0, direct)], x_send.at[s])
        for i in range(len(passing)):
            pass_copy(s, i).wait_send()

    for h in range(pieces):
        out_copy(h).wait()


def shards(acts, grads, act_basis, grad_basis):
    seqs, rows, inputs = acts.shape
    units = grads.shape[2]
    width = inputs // (Y * Z)
    half = width // 2
    pieces = units // PIECE
    stages = seqs * pieces
    length = rows * Y * Z * 2
    dma = pltpu.SemaphoreType.DMA
    return pl.pallas_call(
        functools.partial(kernel, scale=length ** -0.5),
        out_shape=jax.ShapeDtypeStruct((units, half), F32),
        in_specs=[pl.BlockSpec(memory_space=pl.ANY)] * 4,
        out_specs=pl.BlockSpec(memory_space=pl.ANY),
        scratch_shapes=[
            pltpu.VMEM((seqs, Z, rows, width), BF16),
            pltpu.VMEM((seqs, 2 * Y, Z, rows, half), BF16),
            pltpu.VMEM((2, Y * half, 2 * Z * rows), BF16),
            pltpu.VMEM((stages, 2, Z, rows, PIECE), BF16),
            pltpu.VMEM((stages, 3, half, PIECE), BF16),
            pltpu.VMEM((stages, half, PIECE), BF16),
            pltpu.VMEM((stages, 2, half, PIECE), BF16),
            pltpu.VMEM((stages, half, PIECE), F32),
            pltpu.VMEM((stages, half, PIECE), F32),
            pltpu.VMEM((stages, half, PIECE), BF16),
            pltpu.VMEM((stages, half, PIECE), BF16),
            pltpu.VMEM((pieces, half, PIECE), F32),
            pltpu.VMEM((units, half), F32),
            pltpu.VMEM((8, 8, half // 8), F32),
            pltpu.VMEM((8, 8, units // 8), F32),
            pltpu.VMEM((half, 3 * half), BF16),
            pltpu.VMEM((pieces, 2 * PIECE, PIECE), BF16),
            dma((seqs,)), dma((seqs, Z)), dma((stages,)),
            dma((stages,)), dma((stages, Z)),
            dma((stages,)), dma((stages,)),
            dma((seqs,)), dma((seqs, 2 * Y)), dma((seqs, 2)),
            dma((stages,)), dma((stages,)), dma((stages, 2)), dma((stages, 2)),
            dma((stages,)), dma((stages,)), dma((2,)), dma((pieces,)),
        ],
        compiler_params=pltpu.CompilerParams(
            collective_id=0, has_side_effects=True, vmem_limit_bytes=56 << 20
        ),
        name="gathered",
    )(acts, grads, act_basis.transpose(1, 2, 0), grad_basis.transpose(1, 2, 0))


def solution(mesh):
    placed = (
        P(None, "tok", None),
        P(None, "tok", "out"),
        P("tok", None, None),
        P("out", None, None),
    )
    return jax.shard_map(
        shards, mesh=mesh, in_specs=placed, out_specs=P("out", "tok"), check_vma=False
    )
```

```python
import functools

import jax
import jax.numpy as jnp
from jax import lax
from jax.experimental import pallas as pl
from jax.experimental.pallas import tpu as pltpu
from jax.sharding import PartitionSpec as P

MESH = pl.DeviceIdType.MESH
Y, Z, X = 4, 8, 4
PIECE = 256
BF16, F32 = jnp.bfloat16, jnp.float32


def halves(v):
    high = v.astype(BF16)
    return high, (v - high.astype(F32)).astype(BF16)


def dot(a, b):
    return jnp.dot(a, b, preferred_element_type=F32)


def over(a, n):
    return jnp.right_shift(a, n.bit_length() - 1)


def mod(a, n):
    return jnp.bitwise_and(a, n - 1)


def iota(shape, dim):
    return lax.broadcasted_iota(jnp.int32, shape, dim)


def spread(flat, j, size):
    blocks = flat.shape[1]
    first = j * (size // 8)
    repeat = (iota((size, blocks), 1) == first + lax.div(iota((size, blocks), 0), 8)).astype(BF16)
    mine = lax.div(iota((size, 64), 1), 8) == lax.rem(iota((size, 64), 0), 8)
    fold = (lax.rem(iota((64, size), 1), 8) == lax.rem(iota((64, size), 0), 8)).astype(BF16)
    diagonal = lax.div(iota((size, size), 0), 8) == lax.div(iota((size, size), 1), 8)
    parts = []
    for part in halves(flat):
        rows = lax.dot_general(repeat, part, (((1,), (1,)), ((), ())), preferred_element_type=F32)
        rows = jnp.where(mine, rows, 0.0).astype(BF16)
        parts.append(jnp.where(diagonal, dot(rows, fold), 0.0).astype(BF16))
    return parts


def kernel(
    acts, grads, act_basis, grad_basis, out,
    a2, a_all, a_t, g_all, snd, rly, rcv, nxt, own, fin, landed, acc, result, act_flat, grad_flat, act_diag, grad_diag,
    a_send, a_recv, w_send, r_send, g_recv, k_send, k_recv,
    x_send, x_recv, v_send, q_send, q_recv, y_send, y_recv, f_send, f_recv, b_sem, o_sem,
    *, scale,
):
    seqs, rows, _ = acts.shape
    units = grads.shape[2]
    pieces = units // PIECE
    stages = seqs * pieces
    width = a2.shape[-1]
    half = width // 2
    depth = 2 * Z * rows
    tok, place = lax.axis_index("tok"), lax.axis_index("out")
    xh, z, y = mod(tok, 2), mod(over(tok, 2), Z), over(tok, 2 * Z)
    c, xl = mod(place, 2), over(place, 2)
    x = 2 * xh + xl
    sgn = 1 - 2 * c
    chunk = 2 * xl + c

    def dev(xi, yi, zi, ci):
        return ((yi * Z + zi) * 2 + over(xi, 2), 2 * mod(xi, 2) + ci)

    swapped = ((y * Z + z) * 2 + c, 2 * xl + xh)
    stays = xh == c
    moves = jnp.logical_not(stays)

    def remote(src, dst, send, recv, device):
        return pltpu.make_async_remote_copy(
            src_ref=src, dst_ref=dst, send_sem=send, recv_sem=recv,
            device_id=device, device_id_type=MESH,
        )

    def local(src, dst, sem):
        return pltpu.make_async_copy(src, dst, sem)

    def arrived(ref, sem):
        local(ref, ref, sem).wait()

    local(act_basis, act_flat, b_sem.at[0]).start()
    local(grad_basis, grad_flat, b_sem.at[1]).start()
    barrier = pltpu.get_barrier_semaphore()

    def greet(device):
        pl.semaphore_signal(barrier, inc=1, device_id=device, device_id_type=MESH)

    @pl.loop(1, Z)
    def _(d):
        greet(dev(x, y, mod(z + d, Z), c))

    @pl.loop(1, Y)
    def _(d):
        greet(dev(x, mod(y + d, Y), z, c))

    @pl.loop(1, 2 * X)
    def _(d):
        greet(dev(mod(x + over(d, 2), X), y, z, mod(c + d, 2)))

    pl.semaphore_wait(barrier, (Z - 1) + (Y - 1) + (2 * X - 1))

    def a2a_view(s, zt):
        return acts.at[s, :, pl.ds(pl.multiple_of((chunk * Z + zt) * width, width), width)]

    def a2a(s, d):
        for step in {d, Z - d}:
            zt = mod(z + step, Z)
            remote(a2a_view(s, zt), a2.at[s, z], a_send.at[s], a_recv.at[s, z], dev(x, y, zt, c)).start()

    def grads_view(j):
        s, h = over(j, pieces), mod(j, pieces)
        return grads.at[s, :, pl.ds(pl.multiple_of(h * PIECE, PIECE), PIECE)]

    def block(k):
        return mod(z + k * sgn, Z)

    forth, back, partner = dev(x, y, mod(z + sgn, Z), c), dev(x, y, mod(z - sgn, Z), c), dev(x, y, z, 1 - c)

    def ring(j, zz, to, sem):
        return remote(g_all.at[j, c, zz], g_all.at[j, c, zz], sem, g_recv.at[j, zz], to)

    def long(j, k):
        return ring(j, block(-k), forth, r_send.at[j])

    def short(j, k):
        return ring(j, block(k), back, r_send.at[j])

    def across(j):
        return remote(g_all.at[j, c], g_all.at[j, c], k_send.at[j], k_recv.at[j], partner)

    def hop(j, k):
        zz = block(-k)
        arrived(g_all.at[j, c, zz], g_recv.at[j, zz])
        long(j, k).start()
        if k > 0:
            zz = block(k)
            arrived(g_all.at[j, c, zz], g_recv.at[j, zz])
        if k < 3:
            short(j, k).start()

    def last_hop(j):
        zz = block(-4)
        arrived(g_all.at[j, c, zz], g_recv.at[j, zz])
        across(j).start()

    def x_copy(s, d):
        h = mod(c + d, 2)
        cols = pl.ds(pl.multiple_of(h * half, half), half)
        return remote(a2.at[s, :, :, cols], a_all.at[s, 2 * chunk + xh], x_send.at[s],
                      x_recv.at[s, 2 * chunk + xh], dev(mod(x + over(d, 2), X), y, z, h))

    direct = 5

    def xsend(s):
        @pl.loop(0, Z)
        def _(zz):
            arrived(a2.at[s, zz], a_recv.at[s, zz])

        for d in (2, 3, 6, 7):
            x_copy(s, mod(d + 4 * c, 2 * X)).start()
        x_copy(s, 1).start()

        cols = pl.ds(pl.multiple_of(c * half, half), half)
        local(a2.at[s, :, :, cols], a_all.at[s, 2 * chunk + xh], x_recv.at[s, 2 * chunk + xh]).start()

    def slot(dx, ci):
        xi = mod(x + dx, X)
        return 2 * (2 * mod(xi, 2) + ci) + over(xi, 2)

    passing = ((X - 1, 0, 1), (1, 1, X - 1))

    def pass_copy(s, i):
        dx, ci, to = passing[i]
        u = slot(dx, ci)
        return remote(a_all.at[s, u], a_all.at[s, u], v_send.at[s, i], x_recv.at[s, u],
                      dev(mod(x + to, X), y, z, c))

    def xpass(s):
        for i, (dx, ci, to) in enumerate(passing):
            u = slot(dx, ci)
            arrived(a_all.at[s, u], x_recv.at[s, u])
            pass_copy(s, i).start()

    def xrest(s):
        for dx in range(X):
            for ci in range(2):
                if (dx, ci) in ((X - 1, 0), (1, 1)):
                    continue
                u = slot(dx, ci)
                arrived(a_all.at[s, u], x_recv.at[s, u])
        for i, yi in enumerate((far, behind, ahead, y)):
            a_t[s % 2, i * half:(i + 1) * half, :] = a_all[s, pl.ds(2 * yi, 2)].reshape(depth, half).T

    ahead, behind, far = mod(y + sgn, Y), mod(y - sgn, Y), mod(y + 2, Y)
    up, down = dev(x, ahead, z, c), dev(x, behind, z, c)

    def far_copy(j):
        return remote(snd.at[j, 0], rly.at[j], q_send.at[j], q_recv.at[j], up)

    def behind_copy(j):
        return remote(snd.at[j, 1], rcv.at[j, 0], y_send.at[j, 0], y_recv.at[j, 0], down)

    def ahead_copy(j):
        return remote(snd.at[j, 2], rcv.at[j, 1], y_send.at[j, 1], y_recv.at[j, 1], up)

    def multiply(j):
        if j % pieces == 0:
            xrest(j // pieces)

        arrived(g_all.at[j, 1 - c], k_recv.at[j])
        product = dot(a_t[j // pieces % 2], g_all[j].reshape(depth, PIECE))
        snd[j, 0] = product[:half].astype(BF16)
        snd[j, 1] = product[half:2 * half].astype(BF16)
        nxt[j] = product[2 * half:3 * half]
        own[j] = product[3 * half:]
        far_copy(j).start()
        behind_copy(j).start()

    def relay(j):
        arrived(rly.at[j], q_recv.at[j])
        snd[j, 2] = (nxt[j] + rly[j].astype(F32)).astype(BF16)
        ahead_copy(j).start()

    def f_copy(j):
        return remote(fin.at[j], landed.at[j], f_send.at[j], f_recv.at[j], swapped)

    def reduce(j):
        for i in range(2):
            arrived(rcv.at[j, i], y_recv.at[j, i])
        total = own[j] + (rcv[j, 0].astype(F32) + rcv[j, 1].astype(F32))
        fin[j] = total.astype(BF16)

        @pl.when(stays)
        def _():
            local(fin.at[j], landed.at[j], f_recv.at[j]).start()

        @pl.when(moves)
        def _():
            f_copy(j).start()

    def out_copy(h):
        view = pl.ds(h * PIECE, PIECE)
        return local(result.at[view], out.at[view], o_sem.at[h])

    def finish(j):
        s, h = divmod(j, pieces)
        arrived(landed.at[j], f_recv.at[j])
        piece = landed[j]
        high, low = halves(dot(jnp.concatenate([piece, piece], axis=1), grad_diag[h]))
        turned = dot(act_diag[...], jnp.concatenate([high, low, high], axis=0)) * scale
        square = turned * turned
        if s > 0:
            square = acc[h] + square
        if s < seqs - 1:
            acc[h] = square
        else:
            result[h * PIECE:(h + 1) * PIECE, :] = square.T
            out_copy(h).start()

    def drain(j):
        arrived(g_all.at[j, c, pl.ds(0, Z - 1)], r_send.at[j])
        across(j).wait_send()
        far_copy(j).wait_send()
        behind_copy(j).wait_send()
        ahead_copy(j).wait_send()

        @pl.when(moves)
        def _():
            arrived(g_all.at[j, c, 0], w_send.at[j])
            f_copy(j).wait_send()

    def prepare():
        arrived(act_flat, b_sem.at[0])
        arrived(grad_flat, b_sem.at[1])
        high, low = spread(act_flat[...].reshape(64, half // 8), 0, half)
        high, low = high.T, low.T
        for i, part in enumerate((high, high, low)):
            act_diag[:, i * half:(i + 1) * half] = part

        @pl.loop(0, pieces)
        def _(i):
            grad_diag[i, :PIECE], grad_diag[i, PIECE:] = spread(grad_flat[...].reshape(64, units // 8), i, PIECE)

    @pl.loop(0, stages)
    def _(j):
        @pl.when(stays)
        def _():
            local(grads_view(j), g_all.at[j, c, z], g_recv.at[j, z]).start()

        @pl.when(moves)
        def _():
            remote(grads_view(j), g_all.at[j, xh, z], w_send.at[j], g_recv.at[j, z], swapped).start()

    for s in range(seqs):
        local(a2a_view(s, z), a2.at[s, z], a_recv.at[s, z]).start()
    for d in (4, 3, 2, 1):
        a2a(0, d)

    plan = []

    def put(at, step, *args):
        plan.append((at, len(plan), step, args))

    put(0.9, prepare)
    for s, sends, go, through in ((0, (), 0.99, 3.1), (1, (3.0, 3.5, 4.0, 4.4), 5.95, 7.95), (2, (5.1, 5.6, 6.0, 6.4), 8.45, 11.1)):
        for at, d in zip(sends, (4, 3, 2, 1)):
            put(at, a2a, s, d)
        put(go, xsend, s)
        put(through, xpass, s)
    for j in range(stages):
        first = j < pieces
        for k in range(4):
            put(k + j / pieces if first else j - pieces + 1 + 2 * k + (4 - k) / 10, hop, j, k)
        put(4 + j / 10 if first else j + 5, last_hop, j)
        put(4.6 + 0.3 * j if first else j + 5.9, multiply, j)
        put(6.95 + 0.35 * j if first else j + 7.92, relay, j)
        put(8.7 + 0.5 * j if first else j + 10.1, reduce, j)
        put(max(j + 13.2, 17.2 + j / 2), finish, j)
        put(j + 14.5, drain, j)

    for _, _, step, args in sorted(plan, key=lambda call: call[:2]):
        step(*args)

    @pl.loop(0, seqs)
    def _(s):
        arrived(a2.at[s, pl.ds(0, Z - 1)], a_send.at[s])
        arrived(a_all.at[s, pl.ds(0, direct)], x_send.at[s])
        for i in range(len(passing)):
            pass_copy(s, i).wait_send()

    for h in range(pieces):
        out_copy(h).wait()


def shards(acts, grads, act_basis, grad_basis):
    seqs, rows, inputs = acts.shape
    units = grads.shape[2]
    width = inputs // (Y * Z)
    half = width // 2
    pieces = units // PIECE
    stages = seqs * pieces
    length = rows * Y * Z * 2
    dma = pltpu.SemaphoreType.DMA
    return pl.pallas_call(
        functools.partial(kernel, scale=length ** -0.5),
        out_shape=jax.ShapeDtypeStruct((units, half), F32),
        in_specs=[pl.BlockSpec(memory_space=pl.ANY)] * 4,
        out_specs=pl.BlockSpec(memory_space=pl.ANY),
        scratch_shapes=[
            pltpu.VMEM((seqs, Z, rows, width), BF16),
            pltpu.VMEM((seqs, 2 * Y, Z, rows, half), BF16),
            pltpu.VMEM((2, Y * half, 2 * Z * rows), BF16),
            pltpu.VMEM((stages, 2, Z, rows, PIECE), BF16),
            pltpu.VMEM((stages, 3, half, PIECE), BF16),
            pltpu.VMEM((stages, half, PIECE), BF16),
            pltpu.VMEM((stages, 2, half, PIECE), BF16),
            pltpu.VMEM((stages, half, PIECE), F32),
            pltpu.VMEM((stages, half, PIECE), F32),
            pltpu.VMEM((stages, half, PIECE), BF16),
            pltpu.VMEM((stages, half, PIECE), BF16),
            pltpu.VMEM((pieces, half, PIECE), F32),
            pltpu.VMEM((units, half), F32),
            pltpu.VMEM((8, 8, half // 8), F32),
            pltpu.VMEM((8, 8, units // 8), F32),
            pltpu.VMEM((half, 3 * half), BF16),
            pltpu.VMEM((pieces, 2 * PIECE, PIECE), BF16),
            dma((seqs,)), dma((seqs, Z)), dma((stages,)),
            dma((stages,)), dma((stages, Z)),
            dma((stages,)), dma((stages,)),
            dma((seqs,)), dma((seqs, 2 * Y)), dma((seqs, 2)),
            dma((stages,)), dma((stages,)), dma((stages, 2)), dma((stages, 2)),
            dma((stages,)), dma((stages,)), dma((2,)), dma((pieces,)),
        ],
        compiler_params=pltpu.CompilerParams(
            collective_id=0, has_side_effects=True, vmem_limit_bytes=56 << 20
        ),
        name="gathered",
    )(acts, grads, act_basis.transpose(1, 2, 0), grad_basis.transpose(1, 2, 0))


def solution(mesh):
    placed = (
        P(None, "tok", None),
        P(None, "tok", "out"),
        P("tok", None, None),
        P("out", None, None),
    )
    return jax.shard_map(
        shards, mesh=mesh, in_specs=placed, out_specs=P("out", "tok"), check_vma=False
    )
```
